32 devices in a mesh: dp: 8 (over y, x, core), seq: 4 (over z).
Axes of the slice: x: 2, y: 2, z: 4, core: 2. Of those that a mesh axis runs over, the one named last changes fastest.
Arguments:
- enc_states: bfloat16 [8, 256, 4096], P('dp'), may hold values from -6 to 6
- lengths: int32 [8], replicated, may hold values from 1 to 128, as said below
- prompt_owner_sample: int32 [8], replicated, may hold values from 0 to 7, each once
- t5_gain: float32 [4096], replicated, may hold values from 0.5 to 1.5
- t5_in_weight: bfloat16 [2, 4096, 5120], P(None, None, 'seq'), may hold values from -0.09375 to 0.09375
- t5_out_weight: bfloat16 [5120, 4096], P('seq'), may hold values from -0.078125 to 0.078125
- t5_final_gain: float32 [4096], replicated, may hold values from 0.5 to 1.5
- context_weight: bfloat16 [4096, 3072], P('seq', 'dp'), may hold values from -0.09375 to 0.09375
- text_shift: float32 [8, 3072], P('dp'), may hold values from -3 to 3
- text_scale: float32 [8, 3072], P('dp'), may hold values from -0.5 to 0.5
- kv_weight: bfloat16 [3072, 2, 3072], P('dp', None, 'seq'), may hold values from -0.109375 to 0.109375
- text_key_gain: float32 [128], replicated, may hold values from 0.25 to 1.75
- image_query_key_value: bfloat16 [8, 512, 3, 3072], P('dp', 'seq'), may hold values from -6 to 6
- image_qk_gain: float32 [2, 128], replicated, may hold values from 0.25 to 1.75
- proj_weight: bfloat16 [3072, 3072], P('seq', 'dp'), may hold values from -0.109375 to 0.109375
- dora_a: float32 [3072, 64], P('seq'), may hold values from -0.109375 to 0.109375
- dora_b: float32 [64, 3072], P(None, 'dp'), may hold values from -0.375 to 0.375
- magnitude: float32 [3072], P('dp'), may hold values from 0.5 to 2
- grad_out: bfloat16 [8, 512, 3072], P('dp', 'seq'), may hold values from -6 to 6
Outputs:
- image_out: bfloat16 [8, 512, 3072], P('dp', 'seq')
- grad_a: float32 [3072, 64], P('seq')
- grad_b: float32 [64, 3072], P(None, 'dp')
- grad_magnitude: float32 [3072], P('dp')
The draws below stay inside these ranges and needn't reach their ends.
Inputs may be any that keep to these rules, and one draw needn't show every extreme that they name: `lengths`: prompt token counts; in every draw one prompt has exactly 128 tokens. `prompt_owner_sample`: each DiT sample index appears exactly once.
All inputs are finite; a program needn't handle non-finite values.
Results may differ from the reference program's by a relative error of at most 0.024.
Values may be sent and summed in bfloat16 or wider, within the bound.
A program may use at most 128 MiB of HBM per device.

```python
import math
import jax
import jax.numpy as jnp
from jax import lax

D5 = 4096
F5 = 5120
D = 3072
HEADS = 24
HD = 128
RANK = 64
LTXT = 256
BLK = 128
IMG = 512
SAMPLES = 8
N_SEQ = 4


def draw_lengths(key, part):
    length_key, pick_key = jax.random.split(key)
    drawn_lengths = jax.random.randint(length_key, (SAMPLES,), 1, BLK + 1, dtype=jnp.int32)
    longest = jax.random.randint(pick_key, (), 0, SAMPLES, dtype=jnp.int32)
    return jnp.where(jnp.arange(SAMPLES, dtype=jnp.int32) == longest, BLK, drawn_lengths).astype(jnp.int32)


def shard_levels(key, extent, pieces, low, top_value):
    def one(axis_at, shards_of):
        steps = jax.random.uniform(jax.random.fold_in(jax.random.fold_in(key, 6), axis_at), (shards_of,), jnp.float32, low / len(pieces), top_value / len(pieces))
        return jnp.repeat(jnp.exp(steps), extent[axis_at] // shards_of).reshape((-1,) + (1,) * (len(extent) - axis_at - 1))

    factor_of = one(*pieces[0])
    for cut in pieces[1:]:
        factor_of = factor_of * one(*cut)
    return factor_of


def noise(own_key, shape, scale, reach, shards=(), kind=jnp.bfloat16):
    values = jax.random.normal(own_key, shape, jnp.float32) * scale
    if len(shards) > 0:
        values = shard_levels(own_key, shape, shards, -0.22, 0.18) * values
    return jnp.clip(values, min=-reach, max=reach).astype(kind)


def setup_inputs(seed: int = 0) -> dict:
    keys = jax.random.split(jax.random.key(seed), 20)
    enc_states = noise(keys[0], (SAMPLES, LTXT, D5), 1.0, 6.0, ((0, 8),))
    lengths = draw_lengths(jax.random.fold_in(keys[19], 71), 0)
    prompt_owner_sample = jax.random.permutation(keys[2], SAMPLES).astype(jnp.int32)
    t5_gain = jnp.clip(1.0 + 0.1 * jax.random.normal(keys[3], (D5,), jnp.float32), 0.5, 1.5)
    t5_in_weight = noise(keys[4], (2, D5, F5), D5 ** -0.5, 0.09375, ((2, 4),))
    t5_out_weight = noise(keys[5], (F5, D5), F5 ** -0.5, 0.078125, ((0, 4),))
    t5_final_gain = jnp.clip(1.0 + 0.1 * jax.random.normal(keys[6], (D5,), jnp.float32), 0.5, 1.5)
    context_weight = noise(keys[7], (D5, D), D5 ** -0.5, 0.09375, ((0, 4), (1, 8)))
    text_shift = noise(keys[8], (SAMPLES, D), 0.5, 3.0, ((0, 8),), jnp.float32)
    text_scale = jnp.clip(jax.random.uniform(keys[9], (SAMPLES, D), jnp.float32, -0.5, 0.5) * shard_levels(keys[9], (SAMPLES, D), ((0, 8),), -0.4, 0.0), -0.5, 0.5)
    kv_weight = noise(keys[10], (D, 2, D), D ** -0.5, 0.109375, ((0, 8), (2, 4)))
    text_key_gain = jnp.clip(1.0 + 0.15 * jax.random.normal(keys[11], (HD,), jnp.float32), 0.25, 1.75)
    image_query_key_value = noise(keys[12], (SAMPLES, IMG, 3, D), 1.0, 6.0, ((0, 8), (1, 4)))
    image_qk_gain = jnp.clip(1.0 + 0.15 * jax.random.normal(keys[13], (2, HD), jnp.float32), 0.25, 1.75)
    proj_weight = noise(keys[14], (D, D), D ** -0.5, 0.109375, ((0, 4), (1, 8)))
    dora_a = noise(keys[15], (D, RANK), D ** -0.5, 0.109375, ((0, 4),), jnp.float32)
    dora_b = noise(keys[16], (RANK, D), (4 * RANK) ** -0.5, 0.375, ((1, 8),), jnp.float32)
    magnitude = jnp.clip(jnp.exp(math.log(2.0) - 1.3862944 * jax.random.uniform(keys[17], (D,), jnp.float32) ** shard_levels(keys[17], (D,), ((0, 8),), -0.2, 0.2)), 0.5, 2.0)
    grad_out = noise(keys[18], (SAMPLES, IMG, D), 1.0, 6.0, ((0, 8), (1, 4)))
    return {"enc_states": enc_states, "lengths": lengths, "prompt_owner_sample": prompt_owner_sample, "t5_gain": t5_gain, "t5_in_weight": t5_in_weight, "t5_out_weight": t5_out_weight, "t5_final_gain": t5_final_gain, "context_weight": context_weight, "text_shift": text_shift, "text_scale": text_scale, "kv_weight": kv_weight, "text_key_gain": text_key_gain, "image_query_key_value": image_query_key_value, "image_qk_gain": image_qk_gain, "proj_weight": proj_weight, "dora_a": dora_a, "dora_b": dora_b, "magnitude": magnitude, "grad_out": grad_out}


EPSILON = 1e-06

def rms_scale(values, gain):
    return values * lax.rsqrt(lax.optimization_barrier(jnp.mean(values * values, -1, keepdims=True)) + EPSILON) * gain

def reference(enc_states, lengths, prompt_owner_sample, t5_gain, t5_in_weight, t5_out_weight, t5_final_gain, context_weight, text_shift, text_scale, kv_weight, text_key_gain, image_query_key_value, image_qk_gain, proj_weight, dora_a, dora_b, magnitude, grad_out):
    flat_tokens = enc_states.reshape(SAMPLES * LTXT, D5).astype(jnp.float32)
    normed = rms_scale(flat_tokens, t5_gain).astype(jnp.bfloat16)
    gate_proj = jnp.dot(normed, t5_in_weight[0], preferred_element_type=jnp.float32)
    upward = jnp.dot(normed, t5_in_weight[1], preferred_element_type=jnp.float32)
    hidden = (jax.nn.gelu(gate_proj, approximate=True) * upward).astype(jnp.bfloat16)
    hidden_slice = F5 // N_SEQ
    ffn_sum = jnp.zeros((SAMPLES * LTXT, D5), jnp.float32)
    for shard_index in range(N_SEQ):
        partial_value = jnp.dot(hidden[:, shard_index * hidden_slice:(shard_index + 1) * hidden_slice], t5_out_weight[shard_index * hidden_slice:(shard_index + 1) * hidden_slice], preferred_element_type=jnp.float32)
        ffn_sum = ffn_sum + lax.optimization_barrier(partial_value.astype(jnp.bfloat16)).astype(jnp.float32)
    encoded = ((flat_tokens + ffn_sum) * t5_final_gain).astype(jnp.bfloat16)
    feature_slice = D5 // N_SEQ
    context_sum = jnp.zeros((SAMPLES * LTXT, D), jnp.float32)
    for shard_index in range(N_SEQ):
        partial_value = jnp.dot(encoded[:, shard_index * feature_slice:(shard_index + 1) * feature_slice], context_weight[shard_index * feature_slice:(shard_index + 1) * feature_slice], preferred_element_type=jnp.float32)
        context_sum = context_sum + lax.optimization_barrier(partial_value.astype(jnp.bfloat16)).astype(jnp.float32)
    text_embed = context_sum.astype(jnp.bfloat16).reshape(SAMPLES, LTXT, D)
    routed = jnp.zeros_like(text_embed).at[prompt_owner_sample].set(text_embed)
    diffusion_lengths = jnp.zeros_like(lengths).at[prompt_owner_sample].set(lengths)
    routed_values = routed.astype(jnp.float32)
    centre = lax.optimization_barrier(jnp.mean(routed_values, -1, keepdims=True))
    spread = lax.optimization_barrier(jnp.mean((routed_values - centre) * (routed_values - centre), -1, keepdims=True))
    layer_normed = (routed_values - centre) * lax.rsqrt(spread + EPSILON)
    modulated = ((1.0 + text_scale[:, None, :]) * layer_normed + text_shift[:, None, :]).astype(jnp.bfloat16)
    key_value = jnp.dot(modulated.reshape(SAMPLES * LTXT, D), kv_weight.reshape(D, 2 * D), preferred_element_type=jnp.float32).reshape(SAMPLES, LTXT, 2, HEADS, HD)
    prompt_key_rows = rms_scale(key_value[:, :, 0], text_key_gain).astype(jnp.bfloat16)
    prompt_value_rows = key_value[:, :, 1].astype(jnp.bfloat16)
    score_scale = 1.0 / math.sqrt(HD)

    def sample_attention(inputs):
        qkv_rows, keys_text, values_text, prompt_length = inputs
        split_heads = qkv_rows.reshape(IMG, 3, HEADS, HD)
        queries = rms_scale(split_heads[:, 0].astype(jnp.float32), image_qk_gain[0]).astype(jnp.bfloat16)
        key_image = rms_scale(split_heads[:, 1].astype(jnp.float32), image_qk_gain[1]).astype(jnp.bfloat16)
        value_image = split_heads[:, 2]
        key_valid_mask = jnp.arange(LTXT, dtype=jnp.int32) < prompt_length
        text_scores = jnp.einsum('qhd,khd->hqk', queries.astype(jnp.float32), keys_text.astype(jnp.float32)) * score_scale
        text_weight = jnp.where(key_valid_mask[None, None, :], jnp.exp(text_scores), 0.0)
        image_scores = jnp.einsum('qhd,khd->hqk', queries.astype(jnp.float32), key_image.astype(jnp.float32)) * score_scale
        image_weight = jnp.exp(image_scores)
        denominator = lax.optimization_barrier(jnp.sum(text_weight, -1)) + lax.optimization_barrier(jnp.sum(image_weight, -1))
        text_probs = (text_weight / denominator[..., None]).astype(jnp.bfloat16)
        image_probs = (image_weight / denominator[..., None]).astype(jnp.bfloat16)
        mixture = jnp.einsum('hqk,khd->qhd', text_probs.astype(jnp.float32), values_text.astype(jnp.float32))
        mixture = mixture + jnp.einsum('hqk,khd->qhd', image_probs.astype(jnp.float32), value_image.astype(jnp.float32))
        return mixture.astype(jnp.bfloat16).reshape(IMG, D)
    attended_rows = lax.map(sample_attention, (image_query_key_value, prompt_key_rows, prompt_value_rows, diffusion_lengths))
    flat_attended = attended_rows.reshape(SAMPLES * IMG, D)
    direction = proj_weight.astype(jnp.float32) + jnp.dot(dora_a, dora_b, precision=lax.Precision.HIGHEST)
    column_norm = jnp.sqrt(lax.optimization_barrier(jnp.sum(direction * direction, 0)) + EPSILON)
    column_ratio = magnitude / column_norm
    scaled = (direction * column_ratio).astype(jnp.bfloat16)
    head_width = D // N_SEQ
    out_sum = jnp.zeros((SAMPLES * IMG, D), jnp.float32)
    for shard_index in range(N_SEQ):
        partial_value = jnp.dot(flat_attended[:, shard_index * head_width:(shard_index + 1) * head_width], scaled[shard_index * head_width:(shard_index + 1) * head_width], preferred_element_type=jnp.float32)
        out_sum = out_sum + lax.optimization_barrier(partial_value.astype(jnp.bfloat16)).astype(jnp.float32)
    image_out = out_sum.astype(jnp.bfloat16).reshape(SAMPLES, IMG, D)
    weight_grad = jnp.dot(flat_attended.T, grad_out.reshape(SAMPLES * IMG, D), preferred_element_type=jnp.float32)
    grad_magnitude = lax.optimization_barrier(jnp.sum(weight_grad * direction, 0)) / column_norm
    scaled_grad = weight_grad * column_ratio
    grad_a = jnp.dot(scaled_grad, dora_b.T, precision=lax.Precision.HIGHEST)
    grad_b = jnp.dot(dora_a.T, scaled_grad, precision=lax.Precision.HIGHEST)
    return (image_out, grad_a, grad_b, grad_magnitude)
```

```python
import functools
import math

import jax
import jax.numpy as jnp
from jax import lax
from jax.experimental import pallas as pl
from jax.experimental.pallas import tpu as pltpu
from jax.sharding import PartitionSpec as P

HD = 128
MAX_PROMPT = 128
EPSILON = 1e-06


def rms_scale(values, gain):
    return values * lax.rsqrt(jnp.mean(values * values, -1, keepdims=True) + EPSILON) * gain


def attention_kernel(blocks, length_ref, text_gain_ref, image_gain_ref, text_key_ref, text_value_ref, *refs):
    image_refs, out_ref = refs[:blocks], refs[blocks]

    def stacked(kind):
        return jnp.concatenate([ref[kind] for ref in image_refs], 0)

    queries = rms_scale(stacked(0).astype(jnp.float32), image_gain_ref[0:1, :])
    queries = (queries).astype(jnp.bfloat16)
    key_image = rms_scale(stacked(1).astype(jnp.float32), image_gain_ref[1:2, :]).astype(jnp.bfloat16)
    key_text = rms_scale(text_key_ref[...], text_gain_ref[...]).astype(jnp.bfloat16)
    scale = 1.0 / math.sqrt(HD)
    dims = (((1,), (1,)), ((), ()))
    text_scores = lax.dot_general(queries, key_text, dims, preferred_element_type=jnp.float32) * scale
    image_scores = lax.dot_general(queries, key_image, dims, preferred_element_type=jnp.float32) * scale
    position = lax.broadcasted_iota(jnp.int32, text_scores.shape, 1)
    text_weight = jnp.where(position < length_ref[0], jnp.exp(text_scores), 0.0)
    image_weight = jnp.exp(image_scores)
    denominator = jnp.sum(text_weight, -1, keepdims=True) + jnp.sum(image_weight, -1, keepdims=True)
    mixture = jnp.dot(
        text_weight.astype(jnp.bfloat16),
        text_value_ref[...].astype(jnp.bfloat16),
        preferred_element_type=jnp.float32,
    )
    mixture = mixture + jnp.dot(
        image_weight.astype(jnp.bfloat16), stacked(2), preferred_element_type=jnp.float32
    )
    out_ref[...] = (mixture / denominator).astype(jnp.bfloat16)


def attention(length, text_gain, image_gain, key_value, image_blocks):
    blocks = len(image_blocks)
    _, rows, width = image_blocks[0].shape
    heads = width // HD
    text = key_value.shape[0]
    vmem = lambda shape, index: pl.BlockSpec(shape, index)
    return pl.pallas_call(
        functools.partial(attention_kernel, blocks),
        grid=(heads,),
        out_shape=jax.ShapeDtypeStruct((blocks * rows, width), jnp.bfloat16),
        in_specs=[
            pl.BlockSpec(memory_space=pltpu.SMEM),
            vmem((1, HD), lambda h: (0, 0)),
            vmem((2, HD), lambda h: (0, 0)),
            vmem((text, HD), lambda h: (0, h)),
            vmem((text, HD), lambda h: (0, heads + h)),
        ]
        + [vmem((3, rows, HD), lambda h: (0, 0, h))] * blocks,
        out_specs=vmem((blocks * rows, HD), lambda h: (0, h)),
        cost_estimate=pl.CostEstimate(
            flops=4 * heads * blocks * rows * (blocks * rows + text) * HD,
            bytes_accessed=8 * blocks * rows * width,
            transcendentals=heads * blocks * rows * (blocks * rows + text),
        ),
    )(length.reshape(1), text_gain.reshape(1, HD), image_gain, key_value, key_value, *image_blocks)


def on_device(
    enc_states,
    lengths,
    prompt_owner_sample,
    t5_gain,
    t5_in_weight,
    t5_out_weight,
    t5_final_gain,
    context_weight,
    text_shift,
    text_scale,
    kv_weight,
    text_key_gain,
    image_query_key_value,
    image_qk_gain,
    proj_weight,
    dora_a,
    dora_b,
    magnitude,
    grad_out,
):
    seq_rank = lax.axis_index("seq")
    data_rank = lax.axis_index("dp")
    seq_devices = lax.axis_size("seq")
    bf16, f32 = jnp.bfloat16, jnp.float32

    def shifted(values, step):
        return lax.ppermute(values, "seq", [(i, (i + step) % seq_devices) for i in range(seq_devices)])

    image_rows = jnp.transpose(image_query_key_value[0], (1, 0, 2))
    head_width = image_rows.shape[2] // seq_devices

    def heads_of(rank):
        return lax.dynamic_slice_in_dim(image_rows, rank * head_width, head_width, 2)

    image_blocks = [heads_of(seq_rank)] + [
        shifted(heads_of((seq_rank + k) % seq_devices), k) for k in range(1, seq_devices)
    ]

    direction = proj_weight.astype(f32) + jnp.dot(dora_a, dora_b, precision=lax.Precision.HIGHEST)
    column_norm = jnp.sqrt(lax.psum(jnp.sum(direction * direction, 0), "seq") + EPSILON)
    ratio = magnitude / column_norm
    gathered = lax.all_gather(
        jnp.concatenate([(direction * ratio).astype(bf16), (dora_b * ratio).astype(bf16)], 0),
        "dp",
        axis=1,
        tiled=True,
    )
    scaled, scaled_up = gathered[: dora_a.shape[0]], gathered[dora_a.shape[0] :]

    tokens = enc_states[0, :MAX_PROMPT]
    text_length, width_enc = tokens.shape
    feat_width = width_enc // seq_devices
    own_tokens = lax.dynamic_slice_in_dim(tokens, seq_rank * feat_width, feat_width, 1).astype(f32)
    own_final = lax.dynamic_slice_in_dim(t5_final_gain, seq_rank * feat_width, feat_width, 0)
    normed = rms_scale(tokens.astype(f32), t5_gain).astype(bf16)
    gate_proj = jnp.dot(normed, t5_in_weight[0], preferred_element_type=f32)
    upward = jnp.dot(normed, t5_in_weight[1], preferred_element_type=f32)
    hidden = (jax.nn.gelu(gate_proj, approximate=True) * upward).astype(bf16)
    ffn_part = lax.psum_scatter(
        jnp.dot(hidden, t5_out_weight, preferred_element_type=f32).astype(bf16),
        "seq",
        scatter_dimension=1,
        tiled=True,
    ).astype(f32)
    encoded = ((own_tokens + ffn_part) * own_final).astype(bf16)
    context_part = jnp.dot(
        encoded,
        lax.all_gather(context_weight, "dp", axis=1, tiled=True),
        preferred_element_type=f32,
    )
    text_tokens = lax.psum_scatter(context_part.astype(bf16), "seq", scatter_dimension=0, tiled=True)
    routes = prompt_owner_sample == data_rank
    diffusion_length = jnp.sum(jnp.where(routes, lengths, 0))
    prompts = lax.all_gather(text_tokens[None], "dp", axis=0, tiled=True)
    routed = jnp.sum(jnp.where(routes[:, None, None], prompts, jnp.zeros_like(prompts)), 0).astype(f32)
    centre = jnp.mean(routed, -1, keepdims=True)
    spread = jnp.mean((routed - centre) * (routed - centre), -1, keepdims=True)
    layer_normed = (routed - centre) * lax.rsqrt(spread + EPSILON)
    modulated = ((1.0 + text_scale) * layer_normed + text_shift).astype(bf16)
    text_all = lax.all_gather(modulated, "seq", axis=0, tiled=True)
    kv_rows = lax.all_gather(kv_weight.reshape(kv_weight.shape[0], -1), "dp", axis=0, tiled=True)
    key_value = jnp.dot(text_all, kv_rows, preferred_element_type=f32)

    attended = attention(diffusion_length, text_key_gain, image_qk_gain, key_value, image_blocks)

    rows = image_rows.shape[1]
    up_rows = jnp.dot(attended, dora_a.astype(bf16), preferred_element_type=f32).astype(bf16)
    down = lax.dot_general(
        grad_out[0], scaled_up, (((1,), (1,)), ((), ())), preferred_element_type=f32
    ).astype(bf16)
    down_rows = jnp.concatenate([down] + [shifted(down, k) for k in range(1, seq_devices)], 0)
    total, up_total = 0.0, 0.0
    for k in list(range(1, seq_devices)) + [0]:
        block = attended[k * rows : (k + 1) * rows]
        part = jnp.dot(block, scaled, preferred_element_type=f32).astype(bf16)
        up_part = up_rows[k * rows : (k + 1) * rows]
        if k:
            part, up_part = shifted(part, seq_devices - k), shifted(up_part, seq_devices - k)
        total, up_total = total + part.astype(f32), up_total + up_part.astype(f32)
    image_out = total.astype(bf16)

    grad_a = lax.psum(
        lax.dot_general(
            attended, down_rows, (((0,), (0,)), ((), ())), preferred_element_type=f32
        ).astype(bf16),
        "dp",
    ).astype(f32)
    grad_up = lax.dot_general(
        up_total.astype(bf16), grad_out[0], (((0,), (0,)), ((), ())), preferred_element_type=f32
    )
    grad_size = jnp.sum(grad_out[0].astype(f32) * total, 0, keepdims=True)
    column_parts = lax.psum_scatter(
        jnp.concatenate([grad_up, grad_size], 0).astype(bf16), "dp", scatter_dimension=1, tiled=True
    )
    column_sums = lax.psum(column_parts, "seq").astype(f32)
    rank = dora_b.shape[0]
    grad_b = column_sums[:rank] * ratio
    grad_magnitude = column_sums[rank] / magnitude
    return (image_out[None], grad_a, grad_b, grad_magnitude)


def solution(mesh):
    return jax.shard_map(
        on_device,
        mesh=mesh,
        in_specs=(
            P("dp", None, None),
            P(),
            P(),
            P(),
            P(None, None, "seq"),
            P("seq", None),
            P(),
            P("seq", "dp"),
            P("dp", None),
            P("dp", None),
            P("dp", None, "seq"),
            P(),
            P("dp", "seq", None, None),
            P(),
            P("seq", "dp"),
            P("seq", None),
            P(None, "dp"),
            P("dp"),
            P("dp", "seq", None),
        ),
        out_specs=(P("dp", "seq", None), P("seq", None), P(None, "dp"), P("dp")),
        check_vma=False,
    )
```

```python
import functools
import math

import jax
import jax.numpy as jnp
from jax import lax
from jax.experimental import pallas as pl
from jax.experimental.pallas import tpu as pltpu
from jax.sharding import PartitionSpec as P

HD = 128
MAX_PROMPT = 128
EPSILON = 1e-06


def rms_scale(values, gain):
    return values * lax.rsqrt(jnp.mean(values * values, -1, keepdims=True) + EPSILON) * gain


def attention_kernel(blocks, length_ref, text_gain_ref, image_gain_ref, text_key_ref, text_value_ref, *refs):
    image_refs, out_ref = refs[:blocks], refs[blocks]

    def stacked(kind):
        return jnp.concatenate([ref[kind] for ref in image_refs], 0)

    queries = rms_scale(stacked(0).astype(jnp.float32), image_gain_ref[0:1, :])
    queries = (queries).astype(jnp.bfloat16)
    key_image = rms_scale(stacked(1).astype(jnp.float32), image_gain_ref[1:2, :]).astype(jnp.bfloat16)
    key_text = rms_scale(text_key_ref[...], text_gain_ref[...]).astype(jnp.bfloat16)
    scale = 1.0 / math.sqrt(HD)
    dims = (((1,), (1,)), ((), ()))
    text_scores = lax.dot_general(queries, key_text, dims, preferred_element_type=jnp.float32) * scale
    image_scores = lax.dot_general(queries, key_image, dims, preferred_element_type=jnp.float32) * scale
    position = lax.broadcasted_iota(jnp.int32, text_scores.shape, 1)
    text_weight = jnp.where(position < length_ref[0], jnp.exp(text_scores), 0.0)
    image_weight = jnp.exp(image_scores)
    denominator = jnp.sum(text_weight, -1, keepdims=True) + jnp.sum(image_weight, -1, keepdims=True)
    mixture = jnp.dot(
        text_weight.astype(jnp.bfloat16),
        text_value_ref[...].astype(jnp.bfloat16),
        preferred_element_type=jnp.float32,
    )
    mixture = mixture + jnp.dot(
        image_weight.astype(jnp.bfloat16), stacked(2), preferred_element_type=jnp.float32
    )
    out_ref[...] = (mixture / denominator).astype(jnp.bfloat16)


def attention(length, text_gain, image_gain, key_value, image_blocks):
    blocks = len(image_blocks)
    _, rows, width = image_blocks[0].shape
    heads = width // HD
    text = key_value.shape[0]
    vmem = lambda shape, index: pl.BlockSpec(shape, index)
    return pl.pallas_call(
        functools.partial(attention_kernel, blocks),
        grid=(heads,),
        out_shape=jax.ShapeDtypeStruct((blocks * rows, width), jnp.bfloat16),
        in_specs=[
            pl.BlockSpec(memory_space=pltpu.SMEM),
            vmem((1, HD), lambda h: (0, 0)),
            vmem((2, HD), lambda h: (0, 0)),
            vmem((text, HD), lambda h: (0, h)),
            vmem((text, HD), lambda h: (0, heads + h)),
        ]
        + [vmem((3, rows, HD), lambda h: (0, 0, h))] * blocks,
        out_specs=vmem((blocks * rows, HD), lambda h: (0, h)),
        cost_estimate=pl.CostEstimate(
            flops=4 * heads * blocks * rows * (blocks * rows + text) * HD,
            bytes_accessed=8 * blocks * rows * width,
            transcendentals=heads * blocks * rows * (blocks * rows + text),
        ),
    )(length.reshape(1), text_gain.reshape(1, HD), image_gain, key_value, key_value, *image_blocks)


def peers(axis):
    size, rank = lax.axis_size(axis), lax.axis_index(axis)
    return [(k, lax.rem(rank + k, size)) for k in range(1, size)]


def greet(*axes):
    barrier = pltpu.get_barrier_semaphore()
    count = 0
    for axis in axes:
        for _, peer in peers(axis):
            pl.semaphore_signal(
                barrier, inc=1, device_id={axis: peer}, device_id_type=pl.DeviceIdType.MESH
            )
            count += 1
    pl.semaphore_wait(barrier, count)


def send(source, target, send_sem, recv_sem, axis, peer):
    copy = pltpu.make_async_remote_copy(
        src_ref=source,
        dst_ref=target,
        send_sem=send_sem,
        recv_sem=recv_sem,
        device_id={axis: peer},
        device_id_type=pl.DeviceIdType.MESH,
    )
    copy.start()
    return copy


def finish(copies):
    for copy in copies:
        copy.wait()


def sems(count):
    return [pltpu.SemaphoreType.DMA((count,)), pltpu.SemaphoreType.DMA((count,))]


VMEM = pl.BlockSpec(memory_space=pltpu.VMEM)
SMEM = pl.BlockSpec(memory_space=pltpu.SMEM)


def params(collective_id):
    return pltpu.CompilerParams(
        collective_id=collective_id, has_side_effects=True, vmem_limit_bytes=40 * 2**20
    )


def feature_sum_kernel(
    part_ref, tokens_ref, gain_ref, squares_ref, encoded_ref, norm_ref, slots, square_slots, ss, sr, qs, qr
):
    width = tokens_ref.shape[1]
    rank = lax.axis_index("seq")
    greet("seq")
    copies = []
    for k, peer in peers("seq"):
        copies.append(
            send(squares_ref, square_slots.at[k - 1], qs.at[k - 1], qr.at[k - 1], "seq", peer)
        )
        columns = pl.ds(pl.multiple_of(peer * width, 128), width)
        copies.append(
            send(part_ref.at[:, columns], slots.at[k - 1], ss.at[k - 1], sr.at[k - 1], "seq", peer)
        )
    finish(copies)
    own = pl.ds(pl.multiple_of(rank * width, 128), width)
    total = part_ref[:, own].astype(jnp.float32)
    squares = squares_ref[...]
    for k, _ in peers("seq"):
        total = total + slots[k - 1].astype(jnp.float32)
        squares = squares + square_slots[k - 1]
    encoded_ref[...] = ((tokens_ref[...].astype(jnp.float32) + total) * gain_ref[...]).astype(
        encoded_ref.dtype
    )
    norm_ref[...] = jnp.sqrt(squares + EPSILON)


def feature_sum(part, own_tokens, own_gain, squares):
    others = lax.axis_size("seq") - 1
    text, width = own_tokens.shape
    return pl.pallas_call(
        feature_sum_kernel,
        out_shape=[
            jax.ShapeDtypeStruct((text, width), jnp.bfloat16),
            jax.ShapeDtypeStruct(squares.shape, jnp.float32),
        ],
        in_specs=[VMEM] * 4,
        out_specs=[VMEM] * 2,
        scratch_shapes=[
            pltpu.VMEM((others, text, width), jnp.bfloat16),
            pltpu.VMEM((others,) + squares.shape, jnp.float32),
        ]
        + sems(others)
        + sems(others),
        compiler_params=params(1),
    )(part, own_tokens, own_gain, squares)


def route_kernel(
    owner_ref, part_ref, scale_ref, shift_ref, out_ref, slots, stage, prompts, final, ss, sr, ps, pr, fs, fr
):
    rows = stage.shape[0]
    rank, data_rank = lax.axis_index("seq"), lax.axis_index("dp")
    data_devices = lax.axis_size("dp")
    greet("seq", "dp")

    def block(index):
        return pl.ds(pl.multiple_of(index * rows, 16), rows)

    finish(
        [
            send(part_ref.at[block(peer)], slots.at[k - 1], ss.at[k - 1], sr.at[k - 1], "seq", peer)
            for k, peer in peers("seq")
        ]
    )
    total = part_ref[block(rank), :].astype(jnp.float32)
    for k, _ in peers("seq"):
        total = total + slots[k - 1].astype(jnp.float32)
    stage[...] = total.astype(stage.dtype)
    finish(
        [
            send(stage, prompts.at[k - 1], ps.at[k - 1], pr.at[k - 1], "dp", peer)
            for k, peer in peers("dp")
        ]
    )
    routed = jnp.where(owner_ref[data_rank] == data_rank, stage[...].astype(jnp.float32), 0.0)
    for k, _ in peers("dp"):
        prompt = lax.rem(data_rank + data_devices - k, data_devices)
        routed = routed + jnp.where(
            owner_ref[prompt] == data_rank, prompts[k - 1].astype(jnp.float32), 0.0
        )
    centre = jnp.mean(routed, -1, keepdims=True)
    spread = jnp.mean((routed - centre) * (routed - centre), -1, keepdims=True)
    layer_normed = (routed - centre) * lax.rsqrt(spread + EPSILON)
    final[...] = ((1.0 + scale_ref[...]) * layer_normed + shift_ref[...]).astype(final.dtype)
    copies = [
        send(final, out_ref.at[block(rank)], fs.at[k - 1], fr.at[k - 1], "seq", peer)
        for k, peer in peers("seq")
    ]
    out_ref[block(rank), :] = final[...]
    finish(copies)


def route(owner, part, scale, shift):
    others, data_others = lax.axis_size("seq") - 1, lax.axis_size("dp") - 1
    text, width = part.shape
    rows = text // (others + 1)
    return pl.pallas_call(
        route_kernel,
        out_shape=jax.ShapeDtypeStruct((text, width), jnp.bfloat16),
        in_specs=[SMEM] + [VMEM] * 3,
        out_specs=VMEM,
        scratch_shapes=[
            pltpu.VMEM((others, rows, width), jnp.bfloat16),
            pltpu.VMEM((rows, width), jnp.bfloat16),
            pltpu.VMEM((data_others, rows, width), jnp.bfloat16),
            pltpu.VMEM((rows, width), jnp.bfloat16),
        ]
        + sems(others)
        + sems(data_others)
        + sems(others),
        compiler_params=params(2),
    )(owner, part, scale, shift)


def gradient_sum_kernel(
    cols_ref, down_ref, cols_out, down_out, cols_slots, down_slots, stage, stage_slots, down_stage, down_all,
    cs, cr, ds, dr, ss, sr, gs, gr,
):
    data_rank = lax.axis_index("dp")
    greet("seq", "dp")
    copies = []
    for k, peer in peers("dp"):
        copies.append(send(cols_ref.at[peer], cols_slots.at[k - 1], cs.at[k - 1], cr.at[k - 1], "dp", peer))
        copies.append(send(down_ref.at[peer], down_slots.at[k - 1], ds.at[k - 1], dr.at[k - 1], "dp", peer))
    finish(copies)
    cols = cols_ref[data_rank].astype(jnp.float32)
    down = down_ref[data_rank].astype(jnp.float32)
    for k, _ in peers("dp"):
        cols = cols + cols_slots[k - 1].astype(jnp.float32)
        down = down + down_slots[k - 1].astype(jnp.float32)
    stage[...] = cols.astype(stage.dtype)
    down_stage[...] = down.astype(down_stage.dtype)
    copies = [
        send(stage, stage_slots.at[k - 1], ss.at[k - 1], sr.at[k - 1], "seq", peer)
        for k, peer in peers("seq")
    ] + [
        send(down_stage, down_all.at[data_rank], gs.at[k - 1], gr.at[k - 1], "dp", peer)
        for k, peer in peers("dp")
    ]
    down_all[data_rank] = down_stage[...]
    finish(copies)
    cols = stage[...].astype(jnp.float32)
    for k, _ in peers("seq"):
        cols = cols + stage_slots[k - 1].astype(jnp.float32)
    cols_out[...] = cols
    down_out[...] = down_all[...].astype(jnp.float32)


def gradient_sum(cols, down):
    others, data_others = lax.axis_size("seq") - 1, lax.axis_size("dp") - 1
    return pl.pallas_call(
        gradient_sum_kernel,
        out_shape=[
            jax.ShapeDtypeStruct(cols.shape[1:], jnp.float32),
            jax.ShapeDtypeStruct(down.shape, jnp.float32),
        ],
        in_specs=[VMEM] * 2,
        out_specs=[VMEM] * 2,
        scratch_shapes=[
            pltpu.VMEM((data_others,) + cols.shape[1:], jnp.bfloat16),
            pltpu.VMEM((data_others,) + down.shape[1:], jnp.bfloat16),
            pltpu.VMEM(cols.shape[1:], jnp.bfloat16),
            pltpu.VMEM((others,) + cols.shape[1:], jnp.bfloat16),
            pltpu.VMEM(down.shape[1:], jnp.bfloat16),
            pltpu.VMEM(down.shape, jnp.bfloat16),
        ]
        + sems(data_others)
        + sems(data_others)
        + sems(others)
        + sems(data_others),
        compiler_params=params(3),
    )(cols, down)


def on_device(
    enc_states,
    lengths,
    prompt_owner_sample,
    t5_gain,
    t5_in_weight,
    t5_out_weight,
    t5_final_gain,
    context_weight,
    text_shift,
    text_scale,
    kv_weight,
    text_key_gain,
    image_query_key_value,
    image_qk_gain,
    proj_weight,
    dora_a,
    dora_b,
    magnitude,
    grad_out,
):
    seq_rank = lax.axis_index("seq")
    data_rank = lax.axis_index("dp")
    seq_devices = lax.axis_size("seq")
    bf16, f32 = jnp.bfloat16, jnp.float32

    def shifted(values, step):
        return lax.ppermute(values, "seq", [(i, (i + step) % seq_devices) for i in range(seq_devices)])

    kv_own = kv_weight.reshape(kv_weight.shape[0], -1)
    context_columns = lax.all_gather(context_weight, "dp", axis=1, tiled=True)
    kv_rows = lax.all_gather(kv_own, "dp", axis=0, tiled=True)

    image_rows = jnp.transpose(image_query_key_value[0], (1, 0, 2))
    head_width = image_rows.shape[2] // seq_devices

    def heads_of(rank):
        return lax.dynamic_slice_in_dim(image_rows, rank * head_width, head_width, 2)

    image_blocks = [heads_of(seq_rank)] + [
        shifted(heads_of((seq_rank + k) % seq_devices), k) for k in range(1, seq_devices)
    ]

    direction = proj_weight.astype(f32) + jnp.dot(dora_a, dora_b, precision=lax.Precision.HIGHEST)
    squares = jnp.sum(direction * direction, 0, keepdims=True)

    tokens = enc_states[0, :MAX_PROMPT]
    _, width_enc = tokens.shape
    feat_width = width_enc // seq_devices
    own_tokens = lax.dynamic_slice_in_dim(tokens, seq_rank * feat_width, feat_width, 1)
    own_final = lax.dynamic_slice_in_dim(t5_final_gain, seq_rank * feat_width, feat_width, 0)
    normed = rms_scale(tokens.astype(f32), t5_gain).astype(bf16)
    gate_proj = jnp.dot(normed, t5_in_weight[0], preferred_element_type=f32)
    upward = jnp.dot(normed, t5_in_weight[1], preferred_element_type=f32)
    hidden = (jax.nn.gelu(gate_proj, approximate=True) * upward).astype(bf16)
    ffn_part = jnp.dot(hidden, t5_out_weight, preferred_element_type=f32).astype(bf16)
    encoded, column_norm = feature_sum(ffn_part, own_tokens, own_final[None], squares)
    context_part = jnp.dot(encoded, context_columns, preferred_element_type=f32).astype(bf16)
    ratio = magnitude / column_norm[0]
    own_scaled = jnp.concatenate(
        [(direction * ratio).astype(bf16), (dora_b * ratio).astype(bf16)], 0
    )
    own_scaled, context_part = lax.optimization_barrier((own_scaled, context_part))
    gathered = lax.all_gather(own_scaled, "dp", axis=1, tiled=True)
    scaled, scaled_up = gathered[: dora_a.shape[0]], gathered[dora_a.shape[0] :]
    diffusion_length = jnp.sum(jnp.where(prompt_owner_sample == data_rank, lengths, 0))
    text_all = route(prompt_owner_sample, context_part, text_scale, text_shift)

    key_value = jnp.dot(text_all, kv_rows, preferred_element_type=f32)

    attended = attention(diffusion_length, text_key_gain, image_qk_gain, key_value, image_blocks)

    rows = image_rows.shape[1]
    up_rows = jnp.dot(attended, dora_a.astype(bf16), preferred_element_type=f32).astype(bf16)
    down = lax.dot_general(
        grad_out[0], scaled_up, (((1,), (1,)), ((), ())), preferred_element_type=f32
    ).astype(bf16)
    down_rows = jnp.concatenate([down] + [shifted(down, k) for k in range(1, seq_devices)], 0)
    total, up_total = 0.0, 0.0
    for k in list(range(1, seq_devices)) + [0]:
        block = attended[k * rows : (k + 1) * rows]
        part = jnp.dot(block, scaled, preferred_element_type=f32).astype(bf16)
        up_part = up_rows[k * rows : (k + 1) * rows]
        if k:
            part, up_part = shifted(part, seq_devices - k), shifted(up_part, seq_devices - k)
        total, up_total = total + part.astype(f32), up_total + up_part.astype(f32)
    image_out = total.astype(bf16)

    grad_down = lax.dot_general(
        attended, down_rows, (((0,), (0,)), ((), ())), preferred_element_type=f32
    ).astype(bf16)
    grad_up = lax.dot_general(
        up_total.astype(bf16), grad_out[0], (((0,), (0,)), ((), ())), preferred_element_type=f32
    )
    grad_size = jnp.sum(grad_out[0].astype(f32) * total, 0, keepdims=True)
    rank, data_devices = dora_b.shape[0], lax.axis_size("dp")
    spare = jnp.zeros((15, grad_size.shape[1]), f32)
    columns = jnp.concatenate([grad_up, grad_size, spare], 0).astype(bf16)
    columns = columns.reshape(rank + 16, data_devices, -1).transpose(1, 0, 2)
    column_sums, grad_a = gradient_sum(
        columns, grad_down.reshape(data_devices, -1, rank)
    )
    grad_a = grad_a.reshape(-1, rank)
    grad_b = column_sums[:rank] * ratio
    grad_magnitude = column_sums[rank] / magnitude
    return (image_out[None], grad_a, grad_b, grad_magnitude)


def solution(mesh):
    return jax.shard_map(
        on_device,
        mesh=mesh,
        in_specs=(
            P("dp", None, None),
            P(),
            P(),
            P(),
            P(None, None, "seq"),
            P("seq", None),
            P(),
            P("seq", "dp"),
            P("dp", None),
            P("dp", None),
            P("dp", None, "seq"),
            P(),
            P("dp", "seq", None, None),
            P(),
            P("seq", "dp"),
            P("seq", None),
            P(None, "dp"),
            P("dp"),
            P("dp", "seq", None),
        ),
        out_specs=(P("dp", "seq", None), P("seq", None), P(None, "dp"), P("dp")),
        check_vma=False,
    )
```

```python
import functools
import math

import jax
import jax.numpy as jnp
from jax import lax
from jax.experimental import pallas as pl
from jax.experimental.pallas import tpu as pltpu
from jax.sharding import PartitionSpec as P

HD = 128
MAX_PROMPT = 128
EPSILON = 1e-06


def rms_scale(values, gain):
    return values * lax.rsqrt(jnp.mean(values * values, -1, keepdims=True) + EPSILON) * gain


def attention_kernel(blocks, length_ref, text_gain_ref, image_gain_ref, text_key_ref, text_value_ref, *refs):
    image_refs, out_ref = refs[:blocks], refs[blocks]

    def stacked(kind):
        return jnp.concatenate([ref[kind] for ref in image_refs], 0)

    queries = rms_scale(stacked(0).astype(jnp.float32), image_gain_ref[0:1, :])
    queries = (queries).astype(jnp.bfloat16)
    key_image = rms_scale(stacked(1).astype(jnp.float32), image_gain_ref[1:2, :]).astype(jnp.bfloat16)
    key_text = rms_scale(text_key_ref[...], text_gain_ref[...]).astype(jnp.bfloat16)
    scale = 1.0 / math.sqrt(HD)
    dims = (((1,), (1,)), ((), ()))
    text_scores = lax.dot_general(queries, key_text, dims, preferred_element_type=jnp.float32) * scale
    image_scores = lax.dot_general(queries, key_image, dims, preferred_element_type=jnp.float32) * scale
    position = lax.broadcasted_iota(jnp.int32, text_scores.shape, 1)
    text_weight = jnp.where(position < length_ref[0], jnp.exp(text_scores), 0.0)
    image_weight = jnp.exp(image_scores)
    denominator = jnp.sum(text_weight, -1, keepdims=True) + jnp.sum(image_weight, -1, keepdims=True)
    mixture = jnp.dot(
        text_weight.astype(jnp.bfloat16),
        text_value_ref[...].astype(jnp.bfloat16),
        preferred_element_type=jnp.float32,
    )
    mixture = mixture + jnp.dot(
        image_weight.astype(jnp.bfloat16), stacked(2), preferred_element_type=jnp.float32
    )
    out_ref[...] = (mixture / denominator).astype(jnp.bfloat16)


def attention(length, text_gain, image_gain, key_value, image_blocks):
    blocks = len(image_blocks)
    _, rows, width = image_blocks[0].shape
    heads = width // HD
    text = key_value.shape[0]
    vmem = lambda shape, index: pl.BlockSpec(shape, index)
    return pl.pallas_call(
        functools.partial(attention_kernel, blocks),
        grid=(heads,),
        out_shape=jax.ShapeDtypeStruct((blocks * rows, width), jnp.bfloat16),
        in_specs=[
            pl.BlockSpec(memory_space=pltpu.SMEM),
            vmem((1, HD), lambda h: (0, 0)),
            vmem((2, HD), lambda h: (0, 0)),
            vmem((text, HD), lambda h: (0, h)),
            vmem((text, HD), lambda h: (0, heads + h)),
        ]
        + [vmem((3, rows, HD), lambda h: (0, 0, h))] * blocks,
        out_specs=vmem((blocks * rows, HD), lambda h: (0, h)),
        cost_estimate=pl.CostEstimate(
            flops=4 * heads * blocks * rows * (blocks * rows + text) * HD,
            bytes_accessed=8 * blocks * rows * width,
            transcendentals=heads * blocks * rows * (blocks * rows + text),
        ),
    )(length.reshape(1), text_gain.reshape(1, HD), image_gain, key_value, key_value, *image_blocks)


def peers(axis):
    size, rank = lax.axis_size(axis), lax.axis_index(axis)
    return [(k, lax.rem(rank + k, size)) for k in range(1, size)]


def greet(*axes):
    barrier = pltpu.get_barrier_semaphore()
    count = 0
    for axis in axes:
        for _, peer in peers(axis):
            pl.semaphore_signal(
                barrier, inc=1, device_id={axis: peer}, device_id_type=pl.DeviceIdType.MESH
            )
            count += 1
    pl.semaphore_wait(barrier, count)


def send(source, target, send_sem, recv_sem, axis, peer):
    copy = pltpu.make_async_remote_copy(
        src_ref=source,
        dst_ref=target,
        send_sem=send_sem,
        recv_sem=recv_sem,
        device_id={axis: peer},
        device_id_type=pl.DeviceIdType.MESH,
    )
    copy.start()
    return copy


def finish(copies):
    for copy in copies:
        copy.wait()


def sems(count):
    return [pltpu.SemaphoreType.DMA((count,)), pltpu.SemaphoreType.DMA((count,))]


VMEM = pl.BlockSpec(memory_space=pltpu.VMEM)
SMEM = pl.BlockSpec(memory_space=pltpu.SMEM)


def params(collective_id):
    return pltpu.CompilerParams(
        collective_id=collective_id, has_side_effects=True, vmem_limit_bytes=40 * 2**20
    )


def feature_sum_kernel(
    part_ref, tokens_ref, gain_ref, squares_ref, encoded_ref, norm_ref, slots, square_slots, ss, sr, qs, qr
):
    width = tokens_ref.shape[1]
    rank = lax.axis_index("seq")
    greet("seq")
    copies = []
    for k, peer in peers("seq"):
        copies.append(
            send(squares_ref, square_slots.at[k - 1], qs.at[k - 1], qr.at[k - 1], "seq", peer)
        )
        columns = pl.ds(pl.multiple_of(peer * width, 128), width)
        copies.append(
            send(part_ref.at[:, columns], slots.at[k - 1], ss.at[k - 1], sr.at[k - 1], "seq", peer)
        )
    finish(copies)
    own = pl.ds(pl.multiple_of(rank * width, 128), width)
    total = part_ref[:, own].astype(jnp.float32)
    squares = squares_ref[...]
    for k, _ in peers("seq"):
        total = total + slots[k - 1].astype(jnp.float32)
        squares = squares + square_slots[k - 1]
    encoded_ref[...] = ((tokens_ref[...].astype(jnp.float32) + total) * gain_ref[...]).astype(
        encoded_ref.dtype
    )
    norm_ref[...] = jnp.sqrt(squares + EPSILON)


def feature_sum(part, own_tokens, own_gain, squares):
    others = lax.axis_size("seq") - 1
    text, width = own_tokens.shape
    return pl.pallas_call(
        feature_sum_kernel,
        out_shape=[
            jax.ShapeDtypeStruct((text, width), jnp.bfloat16),
            jax.ShapeDtypeStruct(squares.shape, jnp.float32),
        ],
        in_specs=[VMEM] * 4,
        out_specs=[VMEM] * 2,
        scratch_shapes=[
            pltpu.VMEM((others, text, width), jnp.bfloat16),
            pltpu.VMEM((others,) + squares.shape, jnp.float32),
        ]
        + sems(others)
        + sems(others),
        compiler_params=params(1),
    )(part, own_tokens, own_gain, squares)


def route_kernel(
    owner_ref, part_ref, scale_ref, shift_ref, out_ref, slots, stage, prompts, final, ss, sr, ps, pr, fs, fr
):
    rows = stage.shape[0]
    rank, data_rank = lax.axis_index("seq"), lax.axis_index("dp")
    data_devices = lax.axis_size("dp")
    greet("seq", "dp")

    def block(index):
        return pl.ds(pl.multiple_of(index * rows, 16), rows)

    finish(
        [
            send(part_ref.at[block(peer)], slots.at[k - 1], ss.at[k - 1], sr.at[k - 1], "seq", peer)
            for k, peer in peers("seq")
        ]
    )
    total = part_ref[block(rank), :].astype(jnp.float32)
    for k, _ in peers("seq"):
        total = total + slots[k - 1].astype(jnp.float32)
    stage[...] = total.astype(stage.dtype)
    finish(
        [
            send(stage, prompts.at[k - 1], ps.at[k - 1], pr.at[k - 1], "dp", peer)
            for k, peer in peers("dp")
        ]
    )
    routed = jnp.where(owner_ref[data_rank] == data_rank, stage[...].astype(jnp.float32), 0.0)
    for k, _ in peers("dp"):
        prompt = lax.rem(data_rank + data_devices - k, data_devices)
        routed = routed + jnp.where(
            owner_ref[prompt] == data_rank, prompts[k - 1].astype(jnp.float32), 0.0
        )
    centre = jnp.mean(routed, -1, keepdims=True)
    spread = jnp.mean((routed - centre) * (routed - centre), -1, keepdims=True)
    layer_normed = (routed - centre) * lax.rsqrt(spread + EPSILON)
    final[...] = ((1.0 + scale_ref[...]) * layer_normed + shift_ref[...]).astype(final.dtype)
    copies = [
        send(final, out_ref.at[block(rank)], fs.at[k - 1], fr.at[k - 1], "seq", peer)
        for k, peer in peers("seq")
    ]
    out_ref[block(rank), :] = final[...]
    finish(copies)


def route(owner, part, scale, shift):
    others, data_others = lax.axis_size("seq") - 1, lax.axis_size("dp") - 1
    text, width = part.shape
    rows = text // (others + 1)
    return pl.pallas_call(
        route_kernel,
        out_shape=jax.ShapeDtypeStruct((text, width), jnp.bfloat16),
        in_specs=[SMEM] + [VMEM] * 3,
        out_specs=VMEM,
        scratch_shapes=[
            pltpu.VMEM((others, rows, width), jnp.bfloat16),
            pltpu.VMEM((rows, width), jnp.bfloat16),
            pltpu.VMEM((data_others, rows, width), jnp.bfloat16),
            pltpu.VMEM((rows, width), jnp.bfloat16),
        ]
        + sems(others)
        + sems(data_others)
        + sems(others),
        compiler_params=params(2),
    )(owner, part, scale, shift)


def finish_kernel(
    att_ref, weight_ref, dora_ref, down_ref, grad_ref, grad_blocks_ref,
    image_out, size_out, cols_out, down_out,
    parts, stage_r, stage_l, got_r, got_l, up, up_slots, down_slots,
    cols, col_slots, col_stage, col_sums, rows_all, row_slots, row_stage, row_sums,
    size, size_slots, size_stage, size_sums,
    r_s, r_r, l_s, l_r, us, ur, ws, wr, cs, cr, c2s, c2r, as_, ar, a2s, a2r, gs, gr, g2s, g2r,
):
    count = lax.axis_size("seq")
    rank, data_rank = lax.axis_index("seq"), lax.axis_index("dp")
    rows, width = image_out.shape
    depth = att_ref.shape[1]
    half = width // 2
    f32, bf16 = jnp.float32, jnp.bfloat16
    over_rows = (((0,), (0,)), ((), ()))

    def product(k):
        block = att_ref[k * rows : (k + 1) * rows, :]
        for h in range(2):
            columns = slice(h * half, (h + 1) * half)
            parts[k, h] = jnp.dot(block, weight_ref[:depth, columns], preferred_element_type=f32).astype(bf16)

    def link(right, t, h):
        stage, got, ss, rs = (stage_r, got_r, r_s, r_r) if right else (stage_l, got_l, l_s, l_r)
        target = lax.rem(rank + (1 if right else count - 1), count)
        return pltpu.make_async_remote_copy(
            src_ref=stage.at[t - 1, h],
            dst_ref=got.at[t - 1, h],
            send_sem=ss.at[t - 1, h],
            recv_sem=rs.at[t - 1, h],
            device_id={"seq": target},
            device_id_type=pl.DeviceIdType.MESH,
        )

    def chain(t, h):
        for right in (True, False):
            stage, got = (stage_r, got_r) if right else (stage_l, got_l)
            place = rank if right else count - 1 - rank
            part = t if right else count - t

            if t == 1:

                @pl.when(place == 0)
                def _():
                    stage[0, h] = parts[part, h]
                    link(right, 1, h).start()

            else:

                @pl.when(place == 0)
                def _():
                    stage[t - 1, h] = parts[part, h]
                    link(right, t, h).start()

                @pl.when((place >= 1) & (place <= t - 1))
                def _():
                    link(right, t - 1, h).wait_recv()
                    stage[t - 1, h] = (
                        parts[part, h].astype(f32) + got[t - 2, h].astype(f32)
                    ).astype(bf16)
                    link(right, t, h).start()

    greet("seq", "dp")
    done = {0}
    for k in (1, count - 1):
        if k not in done:
            product(k)
            done.add(k)
    for h in range(2):
        chain(1, h)

    ups = jnp.dot(att_ref[...], dora_ref[...], preferred_element_type=f32).astype(bf16)
    for k in range(count):
        up[k] = ups[k * rows : (k + 1) * rows]
    small = []
    for k in range(1, count):
        before = lax.rem(rank + count - k, count)
        small.append(send(up.at[k], up_slots.at[k - 1], us.at[k - 1], ur.at[k - 1], "seq", before))
        after = lax.rem(rank + k, count)
        small.append(send(down_ref, down_slots.at[k - 1], ws.at[k - 1], wr.at[k - 1], "seq", after))
    for t in range(2, count):
        for k in (t, count - t):
            if k not in done:
                product(k)
                done.add(k)
    product(0)
    finish(small)
    up_total = up[0].astype(f32)
    for k in range(1, count):
        up_total = up_total + up_slots[k - 1].astype(f32)
    up_total = up_total.astype(bf16)
    blocks, block_rows = rows_all.shape[0], rows_all.shape[1]
    for j in range(blocks):
        cols[j] = lax.dot_general(
            up_total, grad_blocks_ref[j], over_rows, preferred_element_type=f32
        ).astype(bf16)
    grad_rows = lax.dot_general(att_ref[:rows, :], down_ref[...], over_rows, preferred_element_type=f32)
    for k in range(1, count):
        grad_rows = grad_rows + lax.dot_general(
            att_ref[k * rows : (k + 1) * rows, :], down_slots[k - 1], over_rows, preferred_element_type=f32
        )
    for j in range(blocks):
        rows_all[j] = grad_rows[j * block_rows : (j + 1) * block_rows].astype(bf16)
    first = []
    for k, peer in peers("dp"):
        first.append(send(cols.at[peer], col_slots.at[k - 1], cs.at[k - 1], cr.at[k - 1], "dp", peer))
        first.append(send(rows_all.at[peer], row_slots.at[k - 1], as_.at[k - 1], ar.at[k - 1], "dp", peer))
    second = []
    for t in range(2, count):
        for h in range(2):
            chain(t, h)
        if t == 2:
            finish(first)
            col_total = cols[data_rank].astype(f32)
            row_total = rows_all[data_rank].astype(f32)
            for k, _ in peers("dp"):
                col_total = col_total + col_slots[k - 1].astype(f32)
                row_total = row_total + row_slots[k - 1].astype(f32)
            col_stage[...] = col_total.astype(bf16)
            row_stage[...] = row_total.astype(bf16)
            for k, peer in peers("seq"):
                second.append(send(col_stage, col_sums.at[k - 1], c2s.at[k - 1], c2r.at[k - 1], "seq", peer))
            for k, peer in peers("dp"):
                second.append(
                    send(row_stage, row_sums.at[data_rank], a2s.at[k - 1], a2r.at[k - 1], "dp", peer)
                )
            row_sums[data_rank] = row_stage[...]

    for h in range(2):

        @pl.when(rank >= 1)
        def _():
            link(True, count - 1, h).wait_recv()

        @pl.when(rank <= count - 2)
        def _():
            link(False, count - 1, h).wait_recv()

        columns = slice(h * half, (h + 1) * half)
        total = parts[0, h].astype(f32)
        total = total + jnp.where(rank >= 1, got_r[count - 2, h].astype(f32), 0.0)
        total = total + jnp.where(rank <= count - 2, got_l[count - 2, h].astype(f32), 0.0)
        image_out[:, columns] = total.astype(bf16)
        size[:, columns] = jnp.sum(grad_ref[:, columns].astype(f32) * total, 0, keepdims=True)
    last = [
        send(size, size_slots.at[k - 1], gs.at[k - 1], gr.at[k - 1], "dp", peer) for k, peer in peers("dp")
    ]
    finish(second)
    col_total = col_stage[...].astype(f32)
    for k, _ in peers("seq"):
        col_total = col_total + col_sums[k - 1].astype(f32)
    cols_out[...] = col_total
    down_out[...] = row_sums[...].astype(f32)
    finish(last)
    size_total = size[...]
    for k, _ in peers("dp"):
        size_total = size_total + size_slots[k - 1]
    size_stage[...] = size_total
    finish(
        [
            send(size_stage, size_sums.at[k - 1], g2s.at[k - 1], g2r.at[k - 1], "seq", peer)
            for k, peer in peers("seq")
        ]
    )
    for k, _ in peers("seq"):
        size_total = size_total + size_sums[k - 1]
    size_out[...] = size_total
    for t in range(1, count):
        for h in range(2):

            @pl.when(rank <= t - 1)
            def _():
                link(True, t, h).wait_send()

            @pl.when(count - 1 - rank <= t - 1)
            def _():
                link(False, t, h).wait_send()


def finish_step(attended, gathered, dora, down, grad, grad_blocks):
    count, data_devices = lax.axis_size("seq"), lax.axis_size("dp")
    depth, (rows, width) = attended.shape[1], grad.shape
    rank, own_cols = down.shape[1], grad_blocks.shape[2]
    block_rows = depth // data_devices
    f32, bf16 = jnp.float32, jnp.bfloat16
    halves = (rows, width // 2)
    return pl.pallas_call(
        finish_kernel,
        out_shape=[
            jax.ShapeDtypeStruct((rows, width), bf16),
            jax.ShapeDtypeStruct((1, width), f32),
            jax.ShapeDtypeStruct((rank, own_cols), f32),
            jax.ShapeDtypeStruct((data_devices, block_rows, rank), f32),
        ],
        in_specs=[VMEM] * 6,
        out_specs=[VMEM] * 4,
        scratch_shapes=[
            pltpu.VMEM((count, 2) + halves, bf16),
        ]
        + [pltpu.VMEM((count - 1, 2) + halves, bf16)] * 4
        + [
            pltpu.VMEM((count, rows, rank), bf16),
            pltpu.VMEM((count - 1, rows, rank), bf16),
            pltpu.VMEM((count - 1, rows, rank), bf16),
            pltpu.VMEM((data_devices, rank, own_cols), bf16),
            pltpu.VMEM((data_devices - 1, rank, own_cols), bf16),
            pltpu.VMEM((rank, own_cols), bf16),
            pltpu.VMEM((count - 1, rank, own_cols), bf16),
            pltpu.VMEM((data_devices, block_rows, rank), bf16),
            pltpu.VMEM((data_devices - 1, block_rows, rank), bf16),
            pltpu.VMEM((block_rows, rank), bf16),
            pltpu.VMEM((data_devices, block_rows, rank), bf16),
            pltpu.VMEM((1, width), f32),
            pltpu.VMEM((data_devices - 1, 1, width), f32),
            pltpu.VMEM((1, width), f32),
            pltpu.VMEM((count - 1, 1, width), f32),
        ]
        + [pltpu.SemaphoreType.DMA((count - 1, 2))] * 4
        + sems(count - 1) * 2
        + sems(data_devices - 1)
        + sems(count - 1)
        + sems(data_devices - 1) * 2
        + sems(data_devices - 1)
        + sems(count - 1),
        compiler_params=pltpu.CompilerParams(
            collective_id=3, has_side_effects=True, vmem_limit_bytes=58 * 2**20
        ),
    )(attended, gathered, dora, down, grad, grad_blocks)


def on_device(
    enc_states,
    lengths,
    prompt_owner_sample,
    t5_gain,
    t5_in_weight,
    t5_out_weight,
    t5_final_gain,
    context_weight,
    text_shift,
    text_scale,
    kv_weight,
    text_key_gain,
    image_query_key_value,
    image_qk_gain,
    proj_weight,
    dora_a,
    dora_b,
    magnitude,
    grad_out,
):
    seq_rank = lax.axis_index("seq")
    data_rank = lax.axis_index("dp")
    seq_devices = lax.axis_size("seq")
    bf16, f32 = jnp.bfloat16, jnp.float32

    def shifted(values, step):
        return lax.ppermute(values, "seq", [(i, (i + step) % seq_devices) for i in range(seq_devices)])

    kv_own = kv_weight.reshape(kv_weight.shape[0], -1)
    context_columns = lax.all_gather(context_weight, "dp", axis=1, tiled=True)
    kv_rows = lax.all_gather(kv_own, "dp", axis=0, tiled=True)

    image_rows = jnp.transpose(image_query_key_value[0], (1, 0, 2))
    head_width = image_rows.shape[2] // seq_devices

    def heads_of(rank):
        return lax.dynamic_slice_in_dim(image_rows, rank * head_width, head_width, 2)

    late = seq_devices // 2
    image_blocks = [heads_of(seq_rank)] + [
        None if k == late else shifted(heads_of((seq_rank + k) % seq_devices), k)
        for k in range(1, seq_devices)
    ]

    direction = proj_weight.astype(f32) + jnp.dot(dora_a, dora_b, precision=lax.Precision.HIGHEST)
    squares = jnp.sum(direction * direction, 0, keepdims=True)

    tokens = enc_states[0, :MAX_PROMPT]
    _, width_enc = tokens.shape
    feat_width = width_enc // seq_devices
    own_tokens = lax.dynamic_slice_in_dim(tokens, seq_rank * feat_width, feat_width, 1)
    own_final = lax.dynamic_slice_in_dim(t5_final_gain, seq_rank * feat_width, feat_width, 0)
    normed = rms_scale(tokens.astype(f32), t5_gain).astype(bf16)
    gate_proj = jnp.dot(normed, t5_in_weight[0], preferred_element_type=f32)
    upward = jnp.dot(normed, t5_in_weight[1], preferred_element_type=f32)
    hidden = (jax.nn.gelu(gate_proj, approximate=True) * upward).astype(bf16)
    ffn_part = jnp.dot(hidden, t5_out_weight, preferred_element_type=f32).astype(bf16)
    encoded, column_norm = feature_sum(ffn_part, own_tokens, own_final[None], squares)
    late_heads, encoded = lax.optimization_barrier((heads_of((seq_rank + late) % seq_devices), encoded))
    image_blocks[late] = shifted(late_heads, late)
    context_part = jnp.dot(encoded, context_columns, preferred_element_type=f32).astype(bf16)
    ratio = magnitude / column_norm[0]
    own_scaled = jnp.concatenate(
        [(direction * ratio).astype(bf16), (dora_b * ratio).astype(bf16)], 0
    )
    own_scaled, context_part = lax.optimization_barrier((own_scaled, context_part))
    gathered = lax.all_gather(own_scaled, "dp", axis=1, tiled=True)
    scaled_up = gathered[dora_a.shape[0] :]
    diffusion_length = jnp.sum(jnp.where(prompt_owner_sample == data_rank, lengths, 0))
    text_all = route(prompt_owner_sample, context_part, text_scale, text_shift)

    key_value = jnp.dot(text_all, kv_rows, preferred_element_type=f32)

    attended = attention(diffusion_length, text_key_gain, image_qk_gain, key_value, image_blocks)

    down = lax.dot_general(
        grad_out[0], scaled_up, (((1,), (1,)), ((), ())), preferred_element_type=f32
    ).astype(bf16)
    data_devices = lax.axis_size("dp")
    grad_blocks = grad_out[0].reshape(grad_out.shape[1], data_devices, -1).transpose(1, 0, 2)
    image_out, sizes, column_sums, grad_a = finish_step(
        attended, gathered, dora_a.astype(bf16), down, grad_out[0], grad_blocks
    )
    grad_a = grad_a.reshape(-1, dora_b.shape[0])
    grad_b = column_sums * ratio
    own_cols = magnitude.shape[0]
    grad_magnitude = lax.dynamic_slice_in_dim(sizes[0], data_rank * own_cols, own_cols, 0) / magnitude
    return (image_out[None], grad_a, grad_b, grad_magnitude)


def solution(mesh):
    return jax.shard_map(
        on_device,
        mesh=mesh,
        in_specs=(
            P("dp", None, None),
            P(),
            P(),
            P(),
            P(None, None, "seq"),
            P("seq", None),
            P(),
            P("seq", "dp"),
            P("dp", None),
            P("dp", None),
            P("dp", None, "seq"),
            P(),
            P("dp", "seq", None, None),
            P(),
            P("seq", "dp"),
            P("seq", None),
            P(None, "dp"),
            P("dp"),
            P("dp", "seq", None),
        ),
        out_specs=(P("dp", "seq", None), P("seq", None), P(None, "dp"), P("dp")),
        check_vma=False,
    )
```
